256 devices in a mesh: blk: 32 (over y_hi, z, core), tm: 8 (over y_lo, x).
Axes of the slice: x: 4, y: 4 (y_hi: 2, y_lo: 2; y = y_hi * 2 + y_lo), z: 8, core: 2. Of those that a mesh axis runs over, the one named last changes fastest.
Arguments:
- waveforms: bfloat16 [480, 131072], P(None, ('blk', 'tm')), may hold values from -60 to 60
- templates: bfloat16 [32, 480, 256], P('blk'), may hold values from -6 to 6
- station_mask: int32 [32, 160], P('blk'), may hold values 0 or 1
- channel_order: int32 [480], replicated, may hold values from 0 to 479, each once
Outputs:
- detection: float32 [32, 131072], P(None, ('blk', 'tm'))
The draws below stay inside these ranges and needn't reach their ends.
Inputs may be any that keep to these rules, and one draw needn't show every extreme that they name: `channel_order`: each of 0 to 479 appears once.
All inputs are finite; a program needn't handle non-finite values. No bound on the sum of `station_mask` on one device may be relied on, other than what follows from the above.
Results may differ from the reference program's by a relative error of at most 0.0003.
Values may be sent and summed in bfloat16 or wider, within the bound.
A program may use at most 64 MiB of HBM per device.

```python
import jax
import jax.numpy as jnp
from jax import lax

STATIONS = 160
CHANNELS = 480
TPL_LEN = 256
SLAB = 512
TEMPLATES = 32
TIME = 131072


def draw_waveforms(key, part):
    noise_key = jax.random.fold_in(key, 101)
    level_key = jax.random.fold_in(key, 202)
    gain_key = jax.random.fold_in(key, 303)
    level_count = TIME // 8 + 1
    levels = jnp.exp(1.5 * jax.random.uniform(level_key, (level_count,), jnp.float32, -1.0, 1.0))
    envelope = jnp.repeat(levels, 8)[:TIME]
    gains = jnp.exp(1.2 * jax.random.uniform(gain_key, (CHANNELS, 1), jnp.float32, -1.0, 1.0))
    noise = jnp.clip(jax.random.normal(noise_key, (CHANNELS, TIME), jnp.float32), -4.0, 4.0)
    return (noise * envelope[None, :] * gains).astype(jnp.bfloat16)


def set_ends(values, stream_key, smallest, high):
    longest = values.shape.index(max(values.shape))
    spots = []
    for shift in (0, 1):
        where = [jax.random.randint(jax.random.fold_in(stream_key, axis), (), 0, length) for axis, length in enumerate(values.shape)]
        where[longest] = (where[longest] + shift) % values.shape[longest]
        spots.append(tuple(where))
    return values.at[spots[0]].set(smallest).at[spots[1]].set(high)


def block_levels(rng, dims, pieces, low, high):
    loudness, own = 1.0, jax.random.fold_in(rng, 6)
    for dim, blocks in pieces:
        steps = jnp.exp(jax.random.uniform(jax.random.fold_in(own, dim), (blocks,), jnp.float32, low / len(pieces), high / len(pieces)))
        loudness = loudness * jnp.repeat(steps, dims[dim] // blocks).reshape([-1 if axis == dim else 1 for axis in range(len(dims))])
    return loudness


def gaussian(own_key, shape, width, most, cuts=(), kind=jnp.bfloat16):
    array = jax.random.normal(own_key, shape, jnp.float32) * width
    if len(cuts) > 0:
        array = block_levels(own_key, shape, cuts, -0.22, 0.18) * array
    return jnp.clip(array, min=-most, max=most).astype(kind)


def setup_inputs(seed: int = 0) -> dict:
    key_list = jax.random.split(jax.random.key(seed), 5)
    waveforms = draw_waveforms(jax.random.fold_in(key_list[4], 71), 0)
    templates = gaussian(key_list[1], (TEMPLATES, CHANNELS, TPL_LEN), 1.0, 6.0, ((0, 32),))
    station_mask = set_ends((jax.random.randint(key_list[2], (TEMPLATES, STATIONS), 0, 4) < 3).astype(jnp.int32), jax.random.fold_in(key_list[2], 1), 0, 1)
    channel_order = jax.random.permutation(key_list[3], CHANNELS).astype(jnp.int32)
    return dict(waveforms=waveforms, templates=templates, station_mask=station_mask, channel_order=channel_order)


EPSILON = 1e-05

def station_table(station_mask, channel_order):
    station_of = channel_order // 3
    onehot = (jnp.arange(STATIONS, dtype=jnp.int32)[:, None] == station_of[None, :]).astype(jnp.float32)
    return jnp.dot(station_mask.astype(jnp.float32), onehot, precision=lax.Precision.HIGHEST)

def window_sums(squares, window_len):
    running = squares
    window = 1
    while window < window_len:
        columns = running.shape[1]
        running = running[:, :columns - window] + running[:, window:]
        window = window * 2
    return running

def correlate(masked_row, extended, slab_len, window_len):
    products = lax.dot_general(masked_row, extended, (((0,), (0,)), ((), ())), preferred_element_type=jnp.float32)
    columns = extended.shape[1]
    flattened = jnp.concatenate([products.reshape(-1), jnp.zeros((window_len,), jnp.float32)])
    skewed = flattened.reshape(window_len, columns + 1)[:, :slab_len]
    return lax.optimization_barrier(jnp.sum(skewed, axis=0))

def reference(waveforms, templates, station_mask, channel_order):
    channel_mask = station_table(station_mask, channel_order)
    masked = templates * channel_mask.astype(jnp.bfloat16)[:, :, None]
    tpl_norm = jnp.sqrt(lax.optimization_barrier(jnp.sum(masked.astype(jnp.float32) ** 2, axis=(1, 2))) + EPSILON)
    live = lax.optimization_barrier(jnp.sum(channel_mask, axis=1))
    row_scale = jnp.sqrt(TPL_LEN * live) / tpl_norm
    padded = jnp.pad(waveforms, ((0, 0), (0, TPL_LEN - 1)))
    block_count = TIME // SLAB

    def one_block(block_index):
        begin = (block_index * SLAB).astype(jnp.int32)
        extended = lax.dynamic_slice_in_dim(padded, begin, SLAB + TPL_LEN - 1, 1)
        energy = window_sums(extended.astype(jnp.float32) ** 2, TPL_LEN)
        window_energy = jnp.dot(channel_mask, energy, precision=lax.Precision.HIGHEST)
        dots = lax.map(lambda masked_row: correlate(masked_row, extended, SLAB, TPL_LEN), masked)
        return dots * row_scale[:, None] / jnp.sqrt(window_energy + EPSILON)
    blocks = lax.map(one_block, jnp.arange(block_count, dtype=jnp.int32))
    return jnp.transpose(blocks, (1, 0, 2)).reshape(TEMPLATES, TIME)
```

```python
import jax
import jax.numpy as jnp
from jax import lax
from jax.experimental import pallas as pl
from jax.experimental.pallas import tpu as pltpu
from jax.sharding import PartitionSpec as P

EPSILON = 1e-05
MESH = pl.DeviceIdType.MESH
F32 = jnp.float32
BF16 = jnp.bfloat16

NX, NY, NZ = 4, 4, 8
CHANNELS, WINDOW, SLAB = 480, 256, 512
LANES = 512
SPAN = SLAB + WINDOW
STEP = 16
ROWS = SLAB + STEP
GROUP = 16
PADDED = 640

REACH = {"C": (4, 3), "A": (3, 4), "B": (4, 3), "I": (3, 4)}
ORDER = (
    ("I", 1), ("C", 1), ("A", 1), ("I", 2), ("C", 2), ("B", 1), ("I", 3), ("C", 3), ("A", 2), ("I", 4), ("C", 4),
    ("A", 3), ("B", 2), ("A", 4), ("B", 3), ("B", 4),
)


def padded_lanes(block):
    return jnp.concatenate([block, jnp.zeros((block.shape[0], LANES - block.shape[1]), block.dtype)], axis=1)


def station_onehot(order):
    first = 3 * lax.broadcasted_iota(jnp.int32, (256, CHANNELS), 0)
    hit = jnp.logical_and(order >= first, order < first + 3)
    return padded_lanes(jnp.where(hit, 1.0, 0.0).astype(F32)).astype(BF16)


def window_energy(mask, block):
    wide = block.astype(F32)
    squares = wide * wide
    high = squares.astype(BF16)
    low = (squares - high.astype(F32)).astype(BF16)
    total = jnp.dot(mask, high, preferred_element_type=F32) + jnp.dot(mask, low, preferred_element_type=F32)
    shift = 1
    while shift < WINDOW:
        total = total + pltpu.roll(total, SPAN - shift, 1)
        shift = shift * 2
    return total[:, :SLAB]


def diagonal_sums(partial):
    turned = partial.T.reshape(GROUP, 2, 8, PADDED)
    low, high = turned[:, 0].reshape(GROUP * 8, PADDED), turned[:, 1].reshape(GROUP * 8, PADDED)
    both = low + pltpu.roll(high, PADDED - 8, 1)
    row = lax.broadcasted_iota(jnp.int32, (GROUP * 8, PADDED), 0)
    for bit in (4, 2, 1):
        both = jnp.where((row & bit) != 0, pltpu.roll(both, PADDED - bit, 1), both)
    return jnp.sum(both.reshape(GROUP, 8, PADDED)[:, :, :SLAB], axis=1)


def kernel(wave_ref, tpl_ref, flag_ref, order_ref, out_ref, g, info, xt, own_halo, sib_wave, sib_halo, part, energy, ready, arrived, ssem, rsem):
    blk, tm = lax.axis_index("blk"), lax.axis_index("tm")
    core, z, h = blk % 2, (blk // 2) % NZ, blk // 16
    x, low_y = tm % NX, tm // NX
    y = 2 * h + low_y
    parity, color = (x + y) % 2, (2 * x + y) % 4

    def device(px, py, pz, pc):
        px, py, pz = (px + NX) % NX, (py + NY) % NY, (pz + NZ) % NZ
        return ((py // 2 * NZ + pz) * 2 + pc, py % 2 * NX + px)

    east, west = device(x + 1, y, z, core), device(x - 1, y, z, core)
    north, south = device(x, y + 1, z, core), device(x, y - 1, z, core)
    up, down = device(x, y, z + 1, core), device(x, y, z - 1, core)
    sibling = device(x, y, z, 1 - core)
    mate = device(x, y + 1 - 2 * low_y, z, core)
    cross = device(x, y + 2 * low_y - 1, z, core)
    place = blk * 8 + tm
    after, before = (place + 1) % 256, (place + 255) % 256
    after, before = (after // 8, after % 8), (before // 8, before % 8)

    barrier = pltpu.get_barrier_semaphore()
    friends = (east, west, north, south, up, down, sibling, after, before)
    for friend in friends:
        pl.semaphore_signal(barrier, inc=1, device_id=friend, device_id_type=MESH)

    slots, sent = {}, []

    def copy(name, source, target, to):
        slot = slots.setdefault(name, len(slots))
        return pltpu.make_async_remote_copy(
            src_ref=source, dst_ref=target, send_sem=ssem.at[slot], recv_sem=rsem.at[slot], device_id=to, device_id_type=MESH
        )

    def send(name, source, to, target=None):
        made = copy(name, source, source if target is None else target, to)
        made.start()
        sent.append(made)

    def receive(name, target):
        copy(name, target, target, sibling).wait_recv()

    order = order_ref[...]
    onehot = station_onehot(order)
    flags = jnp.concatenate([flag_ref[...].astype(F32), jnp.zeros((1, 96), F32)], axis=1)
    mask_row = jnp.dot(jnp.broadcast_to(flags, (16, 256)).astype(BF16), onehot, preferred_element_type=F32)[0:1]
    masked = padded_lanes(tpl_ref[...].T) * mask_row.astype(BF16)
    g[h, z] = masked
    wide = masked.astype(F32)
    norm = jnp.sum(jnp.sum(wide * wide, axis=0, keepdims=True), axis=1, keepdims=True)
    live = jnp.sum(mask_row, axis=1, keepdims=True)
    scale = jnp.sqrt(WINDOW * live) / jnp.sqrt(norm + EPSILON)
    info[h, z] = jnp.concatenate(
        [flags[:, :128], flags[:, 128:], jnp.broadcast_to(scale, (1, 128)), jnp.zeros((5, 128), F32)], axis=0
    )
    pl.semaphore_wait(barrier, len(friends))

    def rows(kind, turn=0, flip=0):
        if kind == "C":
            start = 128 + 32 * ((color + turn) % 4)
        else:
            start = 64 * ((parity + flip) % 2) + (32 if kind == "B" else 0)
        return pl.ds(pl.multiple_of(start, 32), 32)

    def piece(kind, hs, zt, turn=0, flip=0):
        if kind == "I":
            return info.at[hs, zt]
        return g.at[hs, zt, rows(kind, turn, flip), :]

    def own_send(kind, hs, tag):
        send((kind, "+", tag), piece(kind, hs, z), up)
        send((kind, "-", tag), piece(kind, hs, z), down)

    cross_turn = 3 - 2 * low_y
    other = 1 - h
    own_send("I", h, 1)
    own_send("C", h, 1)
    send("cross I", info.at[h, z], cross)
    send("cross C", g.at[h, z, rows("C", cross_turn), :], cross)
    send("wave", wave_ref, sibling, sib_wave)
    send("halo", wave_ref.at[:, pl.ds(0, WINDOW)], before, own_halo)
    half = lambda flip: pl.ds(pl.multiple_of(64 * ((parity + flip) % 2), 64), 64)
    send("cross AB", g.at[h, z, half(1), :], cross)
    own_send("A", h, 1)
    own_send("B", h, 1)
    send("cross BA", g.at[h, z, half(0), :], cross)
    for turn in (1, 2, 3):
        send(("cross C", turn), g.at[h, z, rows("C", cross_turn + turn), :], cross)

    xt[0, 0:SLAB, :] = padded_lanes(wave_ref[...].T)
    receive("wave", sib_wave)
    xt[1, 0:SLAB, :] = padded_lanes(sib_wave[...].T)

    receive("cross I", info.at[other, z])
    own_send("I", other, 0)
    receive("cross C", g.at[other, z, rows("C"), :])
    own_send("C", other, 0)
    receive("cross AB", g.at[other, z, half(0), :])
    own_send("A", other, 0)
    own_send("B", other, 0)

    receive("halo", own_halo)
    send("sib halo", own_halo, sibling, sib_halo)
    edge = jnp.where(place == 255, jnp.zeros((), BF16), own_halo[...])
    xt[0, SLAB:SPAN, :] = padded_lanes(edge.T)

    both = pl.ds(0, 2)
    plane = {"C": [], "A": [], "B": []}

    def push(kind, label, to, zt, turn=0):
        send((kind, label), piece(kind, both, zt), to)

    def zstep(kind, r):
        for sign, name, onward in ((1, "+", up), (-1, "-", down)):
            reach = REACH[kind][0 if sign > 0 else 1]
            if r > reach:
                continue
            zt = (z + 8 - sign * r) % NZ
            if r == 1:
                receive((kind, name, 1), piece(kind, h, zt))
                receive((kind, name, 0), piece(kind, other, zt))
            else:
                receive((kind, name, r), piece(kind, both, zt))
            if r < reach:
                send((kind, name, r + 1), piece(kind, both, zt), onward)
            s = 2 * (r - 1) + (0 if sign > 0 else 1)
            if kind == "I":
                continue
            pushes = {
                "C": [("north", north, 3, 0), ("south", south, 1, 0), ("east" if s % 2 else "west", east if s % 2 else west, 2, 0)],
                "A": [("east", east, 0, 1)],
                "B": [("mate", mate, 0, 1) if s % 2 == 0 else ("west", west, 0, 1)],
            }[kind]
            for side, to, turn, flip in pushes:
                label = (kind, side, name, r)
                send(label, piece(kind, both, zt), to)
                plane[kind].append((label, zt, turn, flip))

    def finish(kind):
        for label, zt, turn, flip in plane[kind]:
            receive(label, piece(kind, both, zt, turn, flip))
        if kind == "C":
            for turn in (1, 2, 3):
                receive(("cross C", turn), g.at[other, z, rows("C", turn), :])
        if kind == "A":
            receive("cross BA", g.at[other, z, half(1), :])

    started = set()

    def multiply(start, slab):
        total = None
        for j in (start // STEP, start // STEP + 1):
            tpl = g[:, :, STEP * j : STEP * (j + 1), :].reshape(GROUP * STEP, LANES)
            term = lax.dot_general(
                xt[slab, STEP * j : STEP * j + ROWS, :], tpl, (((1,), (1,)), ((), ())), preferred_element_type=F32
            )
            total = term if total is None else total + term
        if slab in started:
            part[slab, 0:ROWS, :] += total
        else:
            started.add(slab)
            part[slab, 0:ROWS, :] = total
            part[slab, ROWS:PADDED, :] = jnp.zeros((PADDED - ROWS, GROUP * STEP), F32)

    def energies():
        receive("sib halo", sib_halo)
        sib_place = place + 8 - 16 * core
        sib_edge = jnp.where(sib_place == 255, jnp.zeros((), BF16), sib_halo[...])
        xt[1, SLAB:SPAN, :] = padded_lanes(sib_edge.T)
        gathered = jnp.concatenate(
            [info[:, :, 0, :].reshape(GROUP, 128), info[:, :, 1, :].reshape(GROUP, 128)], axis=1
        ).astype(BF16)
        masks = jnp.dot(gathered, onehot, preferred_element_type=F32).astype(BF16)[:, :CHANNELS]
        gains = info[:, :, 2, :].reshape(GROUP, 128)[:, 0:1]
        for slab, block in ((0, jnp.concatenate([wave_ref[...], edge], axis=1)), (1, jnp.concatenate([sib_wave[...], sib_edge], axis=1))):
            energy[slab] = gains / jnp.sqrt(window_energy(masks, block) + EPSILON)

    work = {
        ("C", 4): ["finish C", "energies"],
        ("A", 3): [(128, 0), (160, 0)],
        ("B", 2): [(192, 0), (224, 0)],
        ("A", 4): [(128, 1), (160, 1)],
        ("B", 3): [(192, 1), (224, 1)],
        ("B", 4): ["finish A", (0, 0), (64, 0), (0, 1), (64, 1), "finish B", (32, 1), (96, 1)],
    }
    for item in ORDER:
        zstep(*item)
        for task in work.get(item, ()):
            if task == "energies":
                energies()
            elif isinstance(task, str):
                finish(task[-1])
            else:
                multiply(*task)

    ready[...] = diagonal_sums(part[1]) * energy[1]
    send("result", ready, sibling, arrived)
    multiply(32, 0)
    multiply(96, 0)
    out_ref[core] = diagonal_sums(part[0]) * energy[0]
    receive("result", arrived)
    out_ref[1 - core] = arrived[...]
    for made in sent:
        made.wait_send()


def on_device(waveforms, templates, station_mask, channel_order):
    vmem = pl.BlockSpec(memory_space=pltpu.VMEM)
    slots = 160
    result = pl.pallas_call(
        kernel,
        out_shape=jax.ShapeDtypeStruct((2, GROUP, SLAB), F32),
        in_specs=[vmem] * 4,
        out_specs=vmem,
        scratch_shapes=[
            pltpu.VMEM((2, NZ, WINDOW, LANES), BF16),
            pltpu.VMEM((2, NZ, 8, 128), F32),
            pltpu.VMEM((2, SPAN, LANES), BF16),
            pltpu.VMEM((CHANNELS, WINDOW), BF16),
            pltpu.VMEM((CHANNELS, SLAB), BF16),
            pltpu.VMEM((CHANNELS, WINDOW), BF16),
            pltpu.VMEM((2, PADDED, GROUP * STEP), F32),
            pltpu.VMEM((2, GROUP, SLAB), F32),
            pltpu.VMEM((GROUP, SLAB), F32),
            pltpu.VMEM((GROUP, SLAB), F32),
            pltpu.SemaphoreType.DMA((slots,)),
            pltpu.SemaphoreType.DMA((slots,)),
        ],
        compiler_params=pltpu.CompilerParams(
            collective_id=0, has_side_effects=True, vmem_limit_bytes=50 * 2**20
        ),
    )(waveforms, templates[0], station_mask, channel_order[None, :])
    return jnp.transpose(result, (1, 0, 2)).reshape(2 * GROUP, SLAB)


def solution(mesh):
    placed = (P(None, ("blk", "tm")), P("blk", None, None), P("blk", None), P())
    return jax.shard_map(
        on_device, mesh=mesh, in_specs=placed, out_specs=P(None, ("blk", "tm")), check_vma=False
    )
```

```python
import jax
import jax.numpy as jnp
from jax import lax
from jax.experimental import pallas as pl
from jax.experimental.pallas import tpu as pltpu
from jax.sharding import PartitionSpec as P

EPSILON = 1e-05
MESH = pl.DeviceIdType.MESH
F32 = jnp.float32
BF16 = jnp.bfloat16

NX, NY, NZ = 4, 4, 8
CHANNELS, WINDOW, SLAB = 480, 256, 512
LANES = 512
SPAN = SLAB + WINDOW
STEP = 16
ROWS = SLAB + STEP
GROUP = 16
PADDED = 640

def padded_lanes(block):
    return jnp.concatenate([block, jnp.zeros((block.shape[0], LANES - block.shape[1]), block.dtype)], axis=1)


def station_onehot(order):
    first = 3 * lax.broadcasted_iota(jnp.int32, (256, CHANNELS), 0)
    hit = jnp.logical_and(order >= first, order < first + 3)
    return padded_lanes(jnp.where(hit, 1.0, 0.0).astype(F32)).astype(BF16)


def window_energy(mask, block):
    wide = block.astype(F32)
    squares = wide * wide
    high = squares.astype(BF16)
    low = (squares - high.astype(F32)).astype(BF16)
    total = jnp.dot(mask, high, preferred_element_type=F32) + jnp.dot(mask, low, preferred_element_type=F32)
    shift = 1
    while shift < WINDOW:
        total = total + pltpu.roll(total, SPAN - shift, 1)
        shift = shift * 2
    return total[:, :SLAB]


def diagonal_sums(partial):
    turned = partial.T.reshape(GROUP, 2, 8, PADDED)
    low, high = turned[:, 0].reshape(GROUP * 8, PADDED), turned[:, 1].reshape(GROUP * 8, PADDED)
    both = low + pltpu.roll(high, PADDED - 8, 1)
    row = lax.broadcasted_iota(jnp.int32, (GROUP * 8, PADDED), 0)
    for bit in (4, 2, 1):
        both = jnp.where((row & bit) != 0, pltpu.roll(both, PADDED - bit, 1), both)
    return jnp.sum(both.reshape(GROUP, 8, PADDED)[:, :, :SLAB], axis=1)


def kernel(
    wave_ref, tpl_ref, flag_ref, order_ref, out_ref,
    g, info, xt, tpl_v, wave_v, halo_v, part, energy, result, arrived, ssem, rsem, lsem, late,
):
    blk, tm = lax.axis_index("blk"), lax.axis_index("tm")
    core, z, h = blk % 2, (blk // 2) % NZ, blk // 16
    x, low_y = tm % NX, tm // NX
    y = 2 * h + low_y
    other = 1 - h
    color = (x + 2 * y) % 4

    def device(px, py, pz, pc):
        px, py, pz = (px + NX) % NX, (py + NY) % NY, (pz + NZ) % NZ
        return ((py // 2 * NZ + pz) * 2 + pc, py % 2 * NX + px)

    cross_y = y + 2 * low_y - 1
    line = {dz: device(x, y, z + dz, core) for dz in (1, -1, 2, -2, 3, -3, 4)}
    cross = {dz: device(x, cross_y, z + dz, core) for dz in (0, 1, -1, 2, -2, 3, -3, 4)}
    east, west = device(x + 1, y, z, core), device(x - 1, y, z, core)
    mate = device(x, y + 1 - 2 * low_y, z, core)
    sibling = device(x, y, z, 1 - core)
    place = blk * 8 + tm
    after, before = (place + 1) % 256, (place + 255) % 256
    after, before = (after // 8, after % 8), (before // 8, before % 8)

    load_tpl = pltpu.make_async_copy(tpl_ref, tpl_v, lsem.at[0])
    load_wave = pltpu.make_async_copy(wave_ref, wave_v.at[core], lsem.at[1])
    load_tpl.start()
    load_wave.start()

    last_in_run = jnp.logical_and(x == NX - 1, low_y == 1)
    first_in_run = jnp.logical_and(x == 0, low_y == 0)
    barrier = pltpu.get_barrier_semaphore()
    friends = list(line.values()) + list(cross.values()) + [east, west, mate]
    for friend in friends:
        pl.semaphore_signal(barrier, inc=1, device_id=friend, device_id_type=MESH)

    @pl.when(core == 0)
    def _():
        pl.semaphore_signal(barrier, inc=1, device_id=sibling, device_id_type=MESH)

    @pl.when(jnp.logical_or(core == 0, jnp.logical_not(last_in_run)))
    def _():
        pl.semaphore_signal(barrier, inc=1, device_id=after, device_id_type=MESH)

    @pl.when(jnp.logical_or(core == 0, jnp.logical_not(first_in_run)))
    def _():
        pl.semaphore_signal(barrier, inc=1, device_id=before, device_id_type=MESH)

    slots, sent = {}, []

    def copy(name, source, target, to):
        slot = slots.setdefault(name, len(slots))
        return pltpu.make_async_remote_copy(
            src_ref=source, dst_ref=target, send_sem=ssem.at[slot], recv_sem=rsem.at[slot], device_id=to, device_id_type=MESH
        )

    def send(name, source, to):
        made = copy(name, source, source, to)
        made.start()
        sent.append(made)

    def receive(name, target):
        copy(name, target, target, sibling).wait_recv()

    order = order_ref[...]
    onehot = station_onehot(order)
    flags = jnp.concatenate([flag_ref[...].astype(F32), jnp.zeros((1, 96), F32)], axis=1)
    mask_row = jnp.dot(jnp.broadcast_to(flags, (16, 256)).astype(BF16), onehot, preferred_element_type=F32)[0:1]
    load_tpl.wait()
    masked = padded_lanes(tpl_v[...].T) * mask_row.astype(BF16)
    g[h, z] = masked
    wide = masked.astype(F32)
    norm = jnp.sum(jnp.sum(wide * wide, axis=0, keepdims=True), axis=1, keepdims=True)
    live = jnp.sum(mask_row, axis=1, keepdims=True)
    scale = jnp.sqrt(WINDOW * live) / jnp.sqrt(norm + EPSILON)
    info[h, z] = jnp.concatenate(
        [flags[:, :128], flags[:, 128:], jnp.broadcast_to(scale, (1, 128)), jnp.zeros((5, 128), F32)], axis=0
    )
    number = lambda yes: jnp.where(yes, 1, 0)
    pl.semaphore_wait(
        barrier,
        len(friends) + core + number(jnp.logical_or(core == 1, jnp.logical_not(last_in_run)))
        + number(jnp.logical_or(core == 1, jnp.logical_not(first_in_run))),
    )

    @pl.when(core == 1)
    def _():
        pl.semaphore_signal(late.at[0], inc=1, device_id=sibling, device_id_type=MESH)

    @pl.when(jnp.logical_and(core == 1, last_in_run))
    def _():
        pl.semaphore_signal(late.at[1], inc=1, device_id=after, device_id_type=MESH)

    def rows(kind, turn):
        return pl.ds(pl.multiple_of(128 * kind + 32 * ((color + turn) % 4), 32), 32)

    def piece(kind, hs, dz, turn=0):
        return g.at[hs, (z - dz + NZ) % NZ, rows(kind, turn), :]

    both = pl.ds(0, 2)
    for kind in (0, 1):
        for dz in (2, -2, 1, -1):
            send((kind, "line", dz), piece(kind, h, 0), line[dz])
            send((kind, "cross", dz), piece(kind, h, 0, 2), cross[dz])
        if kind == 0:
            for dz in line:
                send(("info", "line", dz), info.at[h, z], line[dz])
            for dz in cross:
                send(("info", "cross", dz), info.at[h, z], cross[dz])
    send("cross whole", g.at[h, z], cross[0])

    load_wave.wait()
    wave_copy = copy("wave", wave_v.at[core], wave_v.at[core], sibling)
    halo_copy = copy("halo", wave_v.at[core, :, pl.ds(0, WINDOW)], halo_v.at[core], before)
    edge_copy = copy("edge", wave_v.at[core, :, pl.ds(0, WINDOW)], halo_v.at[1 - core], before)
    crossing = jnp.logical_and(first_in_run, core == 0)

    @pl.when(core == 1)
    def _():
        wave_copy.start()

    @pl.when(jnp.logical_not(first_in_run))
    def _():
        halo_copy.start()

    @pl.when(jnp.logical_and(first_in_run, core == 1))
    def _():
        edge_copy.start()

    plane = {0: [], 1: []}

    def zstep(kind, dz):
        if abs(dz) <= 2:
            receive((kind, "line", dz), piece(kind, h, dz))
            receive((kind, "cross", dz), piece(kind, other, dz))
        else:
            receive((kind, "far", dz), piece(kind, both, dz))
        sign = 1 if dz > 0 else -1
        if abs(dz) == 2:
            send((kind, "far", 3 * sign), piece(kind, both, dz), line[sign])
            if sign == (1 if kind == 0 else -1):
                send((kind, "far", 4), piece(kind, both, dz), line[2 * sign])
        to, label = (mate, "mate") if kind == 0 or dz not in (1, 2, 3) else (cross[0], "cross y")
        for label, to, turn in (("east", east, 3), ("west", west, 1), (label, to, 2)):
            send((kind, label, "plane", dz), piece(kind, both, dz), to)
            plane[kind].append(((kind, label, "plane", dz), dz, turn))

    for step in ((0, 2), (0, -2), (0, 1), (0, -1), (1, 2), (1, -2), (1, 1), (1, -1), (0, 3), (0, -3), (0, 4), (1, 3), (1, -3), (1, 4)):
        zstep(*step)

    @pl.when(core == 0)
    def _():
        pl.semaphore_wait(late.at[0], 1)
        wave_copy.start()

    @pl.when(crossing)
    def _():
        pl.semaphore_wait(late.at[1], 1)
        edge_copy.start()

    @pl.when(jnp.logical_not(last_in_run))
    def _():
        receive("halo", halo_v.at[core])

    @pl.when(last_in_run)
    def _():
        receive("edge", halo_v.at[core])

    send("sib halo", halo_v.at[core], sibling)

    @pl.when(core == 1)
    def _():
        receive("wave", wave_v.at[0])
        receive("sib halo", halo_v.at[0])

    for dz in line:
        receive(("info", "line", dz), info.at[h, (z - dz + NZ) % NZ])
    for dz in cross:
        receive(("info", "cross", dz), info.at[other, (z - dz + NZ) % NZ])
    gathered = jnp.concatenate(
        [info[:, :, 0, :].reshape(GROUP, 128), info[:, :, 1, :].reshape(GROUP, 128)], axis=1
    ).astype(BF16)
    masks = jnp.dot(gathered, onehot, preferred_element_type=F32).astype(BF16)[:, :CHANNELS]
    gains = info[:, :, 2, :].reshape(GROUP, 128)[:, 0:1]

    def prepare(slab):
        wave = wave_v[slab]
        end = place + 8 * (slab - core) == 255
        edge = jnp.where(end, jnp.zeros((), BF16), halo_v[slab])
        xt[slab, 0:SLAB, :] = padded_lanes(wave.T)
        xt[slab, SLAB:SPAN, :] = padded_lanes(edge.T)
        total = window_energy(masks, jnp.concatenate([wave, edge], axis=1))
        energy[slab] = gains / jnp.sqrt(total + EPSILON)

    def multiply(kind, turn, slab, first):
        start = 128 * kind + 32 * ((color + turn) % 4)
        total = None
        for half in (0, STEP):
            at = pl.multiple_of(start + half, STEP)
            tpl = g[:, :, pl.ds(at, STEP), :].reshape(GROUP * STEP, LANES)
            term = lax.dot_general(
                xt[slab, pl.ds(at, ROWS), :], tpl, (((1,), (1,)), ((), ())), preferred_element_type=F32
            )
            total = term if total is None else total + term
        if first:
            part[slab, 0:ROWS, :] = total
            part[slab, ROWS:PADDED, :] = jnp.zeros((PADDED - ROWS, GROUP * STEP), F32)
        else:
            part[slab, 0:ROWS, :] += total

    def finish(kind, turn):
        for name, dz, its in plane[kind]:
            if its == turn:
                receive(name, piece(kind, both, dz, turn))

    prepare(0)
    receive("cross whole", g.at[other, z])
    for kind in (0, 1):
        for turn in (0, 2, 1, 3):
            finish(kind, turn)
            multiply(kind, turn, 0, (kind, turn) == (0, 0))
    result[0] = diagonal_sums(part[0]) * energy[0]
    result_copy = copy("result", result.at[1 - core], arrived, sibling)

    @pl.when(core == 1)
    def _():
        result_copy.start()

    @pl.when(core == 0)
    def _():
        receive("wave", wave_v.at[1])
        receive("sib halo", halo_v.at[1])

    prepare(1)
    for kind in (0, 1):
        for turn in (0, 2, 1, 3):
            multiply(kind, turn, 1, (kind, turn) == (0, 0))
    result[1] = diagonal_sums(part[1]) * energy[1]

    @pl.when(core == 0)
    def _():
        result_copy.start()

    out_ref[core] = result[core]
    receive("result", arrived)
    out_ref[1 - core] = arrived[...]
    for made in sent:
        made.wait_send()
    wave_copy.wait_send()
    result_copy.wait_send()

    @pl.when(jnp.logical_not(first_in_run))
    def _():
        halo_copy.wait_send()

    @pl.when(first_in_run)
    def _():
        edge_copy.wait_send()


def on_device(waveforms, templates, station_mask, channel_order):
    vmem = pl.BlockSpec(memory_space=pltpu.VMEM)
    hbm = pl.BlockSpec(memory_space=pl.ANY)
    slots = 96
    result = pl.pallas_call(
        kernel,
        out_shape=jax.ShapeDtypeStruct((2, GROUP, SLAB), F32),
        in_specs=[hbm, hbm, vmem, vmem],
        out_specs=vmem,
        scratch_shapes=[
            pltpu.VMEM((2, NZ, WINDOW, LANES), BF16),
            pltpu.VMEM((2, NZ, 8, 128), F32),
            pltpu.VMEM((2, SPAN, LANES), BF16),
            pltpu.VMEM((CHANNELS, WINDOW), BF16),
            pltpu.VMEM((2, CHANNELS, SLAB), BF16),
            pltpu.VMEM((2, CHANNELS, WINDOW), BF16),
            pltpu.VMEM((2, PADDED, GROUP * STEP), F32),
            pltpu.VMEM((2, GROUP, SLAB), F32),
            pltpu.VMEM((2, GROUP, SLAB), F32),
            pltpu.VMEM((GROUP, SLAB), F32),
            pltpu.SemaphoreType.DMA((slots,)),
            pltpu.SemaphoreType.DMA((slots,)),
            pltpu.SemaphoreType.DMA((2,)),
            pltpu.SemaphoreType.REGULAR((2,)),
        ],
        compiler_params=pltpu.CompilerParams(
            collective_id=0, has_side_effects=True, vmem_limit_bytes=50 * 2**20
        ),
    )(waveforms, templates[0], station_mask, channel_order[None, :])
    return jnp.transpose(result, (1, 0, 2)).reshape(2 * GROUP, SLAB)


def solution(mesh):
    placed = (P(None, ("blk", "tm")), P("blk", None, None), P("blk", None), P())
    return jax.shard_map(
        on_device, mesh=mesh, in_specs=placed, out_specs=P(None, ("blk", "tm")), check_vma=False
    )
```

```python
import jax
import jax.numpy as jnp
from jax import lax
from jax.experimental import pallas as pl
from jax.experimental.pallas import tpu as pltpu
from jax.sharding import PartitionSpec as P

EPSILON = 1e-05
MESH = pl.DeviceIdType.MESH
F32 = jnp.float32
BF16 = jnp.bfloat16

NX, NY, NZ = 4, 4, 8
CHANNELS, WINDOW, SLAB = 480, 256, 512
LANES = 512
SPAN = SLAB + WINDOW
STEP = 16
ROWS = SLAB + STEP
GROUP = 16
PADDED = 640

def padded_lanes(block):
    return jnp.concatenate([block, jnp.zeros((block.shape[0], LANES - block.shape[1]), block.dtype)], axis=1)


def station_onehot(order):
    first = 3 * lax.broadcasted_iota(jnp.int32, (256, CHANNELS), 0)
    hit = jnp.logical_and(order >= first, order < first + 3)
    return padded_lanes(jnp.where(hit, 1.0, 0.0).astype(F32)).astype(BF16)


def window_energy(mask, block):
    wide = block.astype(F32)
    squares = wide * wide
    high = squares.astype(BF16)
    low = (squares - high.astype(F32)).astype(BF16)
    total = jnp.dot(mask, high, preferred_element_type=F32) + jnp.dot(mask, low, preferred_element_type=F32)
    shift = 1
    while shift < WINDOW:
        total = total + pltpu.roll(total, SPAN - shift, 1)
        shift = shift * 2
    return total[:, :SLAB]


def diagonal_sums(partial):
    turned = partial.T.reshape(GROUP, 2, 8, PADDED)
    low, high = turned[:, 0].reshape(GROUP * 8, PADDED), turned[:, 1].reshape(GROUP * 8, PADDED)
    both = low + pltpu.roll(high, PADDED - 8, 1)
    row = lax.broadcasted_iota(jnp.int32, (GROUP * 8, PADDED), 0)
    for bit in (4, 2, 1):
        both = jnp.where((row & bit) != 0, pltpu.roll(both, PADDED - bit, 1), both)
    return jnp.sum(both.reshape(GROUP, 8, PADDED)[:, :, :SLAB], axis=1)


def kernel(
    wave_ref, tpl_ref, flag_ref, order_ref, out_ref,
    g, info, xt, order_v, flag_v, tpl_v, wave_v, halo_v, part, energy, result, arrived, ssem, rsem, lsem,
):
    blk, tm = lax.axis_index("blk"), lax.axis_index("tm")
    core, z, h = blk % 2, (blk // 2) % NZ, blk // 16
    x, low_y = tm % NX, tm // NX
    y = 2 * h + low_y
    other = 1 - h
    colors = ((x + 2 * y) % 4, (2 * x + y) % 4)
    cross_turns = (2, 3 - 2 * low_y)

    def device(px, py, pz, pc):
        px, py, pz = (px + NX) % NX, (py + NY) % NY, (pz + NZ) % NZ
        return ((py // 2 * NZ + pz) * 2 + pc, py % 2 * NX + px)

    line = {dz: device(x, y, z + dz, core) for dz in (1, -1, 2, -2)}
    cross = device(x, y + 2 * low_y - 1, z, core)
    east, west = device(x + 1, y, z, core), device(x - 1, y, z, core)
    north, south = device(x, y + 1, z, core), device(x, y - 1, z, core)
    mate = device(x, y + 1 - 2 * low_y, z, core)
    sibling = device(x, y, z, 1 - core)
    place = blk * 8 + tm
    after, before = (place + 1) % 256, (place + 255) % 256
    after, before = (after // 8, after % 8), (before // 8, before % 8)

    load_tpl = pltpu.make_async_copy(tpl_ref, tpl_v, lsem.at[0])
    load_wave = pltpu.make_async_copy(wave_ref, wave_v.at[0], lsem.at[1])
    load_order = pltpu.make_async_copy(order_ref, order_v, lsem.at[2])
    load_flags = pltpu.make_async_copy(flag_ref, flag_v, lsem.at[3])
    load_order.start()
    load_flags.start()
    load_tpl.start()
    load_wave.start()

    barrier = pltpu.get_barrier_semaphore()
    friends = list(line.values()) + [cross, east, west, mate, sibling, after, before]
    for friend in friends:
        pl.semaphore_signal(barrier, inc=1, device_id=friend, device_id_type=MESH)

    slots, sent = {}, []

    def copy(name, source, target, to):
        slot = slots.setdefault(name, len(slots))
        return pltpu.make_async_remote_copy(
            src_ref=source, dst_ref=target, send_sem=ssem.at[slot], recv_sem=rsem.at[slot], device_id=to, device_id_type=MESH
        )

    def send(name, source, to, target=None):
        made = copy(name, source, source if target is None else target, to)
        made.start()
        sent.append(made)

    def receive(name, target):
        copy(name, target, target, sibling).wait_recv()

    load_order.wait()
    load_flags.wait()
    order = order_v[...]
    onehot = station_onehot(order)
    flags = jnp.concatenate([flag_v[...].astype(F32), jnp.zeros((1, 96), F32)], axis=1)
    mask_row = jnp.dot(jnp.broadcast_to(flags, (16, 256)).astype(BF16), onehot, preferred_element_type=F32)[0:1]
    load_tpl.wait()
    masked = padded_lanes(tpl_v[...].T) * mask_row.astype(BF16)
    g[h, z] = masked
    wide = masked.astype(F32)
    norm = jnp.sum(jnp.sum(wide * wide, axis=0, keepdims=True), axis=1, keepdims=True)
    live = jnp.sum(mask_row, axis=1, keepdims=True)
    scale = jnp.sqrt(WINDOW * live) / jnp.sqrt(norm + EPSILON)
    info[h, z] = jnp.concatenate(
        [flags[:, :128], flags[:, 128:], jnp.broadcast_to(scale, (1, 128)), jnp.zeros((5, 128), F32)], axis=0
    )
    load_wave.wait()
    pl.semaphore_wait(barrier, len(friends))

    def rows(kind, turn):
        return pl.ds(pl.multiple_of(128 * kind + 32 * ((colors[kind] + turn) % 4), 32), 32)

    def piece(kind, hs, dz, turn=0):
        return g.at[hs, (z - dz + NZ) % NZ, rows(kind, turn), :]

    both = pl.ds(0, 2)
    send("halo", wave_v.at[0, :, pl.ds(0, WINDOW)], before, halo_v.at[0])
    send("wave", wave_v.at[0], sibling, wave_v.at[1])
    for kind in (0, 1):
        send(("cross", kind, 0), piece(kind, h, 0, cross_turns[kind]), cross)
    send(("cross", "info"), info.at[h, z], cross)

    def to_line(kind, hs, tag):
        for dz in (2, -2, 1, -1):
            if kind == "info":
                send((kind, tag, dz), info.at[hs, z], line[dz])
            else:
                send((kind, tag, dz), piece(kind, hs, 0), line[dz])

    to_line(0, h, "own")
    to_line("info", h, "own")
    to_line(1, h, "own")
    for turn in (1, 2, 3):
        for kind in (0, 1):
            send(("cross", kind, turn), piece(kind, h, 0, cross_turns[kind] + turn), cross)

    plane = {0: [], 1: []}

    def part_of(kind, hs, dz):
        return info.at[hs, (z - dz + NZ) % NZ] if kind == "info" else piece(kind, hs, dz)

    def zstep(kind, dz):
        if abs(dz) <= 2:
            receive((kind, "own", dz), part_of(kind, h, dz))
            receive((kind, "other", dz), part_of(kind, other, dz))
        else:
            receive((kind, "far", dz), part_of(kind, both, dz))
        sign = 1 if dz > 0 else -1
        if abs(dz) == 2:
            send((kind, "far", 3 * sign), part_of(kind, both, dz), line[sign])
            if sign == (1 if kind == 0 else -1):
                send((kind, "far", 4), part_of(kind, both, dz), line[2 * sign])
        if kind == "info":
            return
        if kind == 0:
            pushes = (("east", east, 3), ("west", west, 1), (("cross y", cross, 2) if dz in (2, 1) else ("mate", mate, 2)))
        else:
            third = ("west", west, 2) if dz in (2, -1) else ("east", east, 2)
            pushes = (("north", north, 3), ("south", south, 1), third)
        for label, to, turn in pushes:
            send((kind, label, "plane", dz), piece(kind, both, dz), to)
            plane[kind].append(((kind, label, "plane", dz), dz, turn))

    def multiply(kind, turn, slab, first=False):
        start = 128 * kind + 32 * ((colors[kind] + turn) % 4)
        total = None
        for half in (0, STEP):
            at = pl.multiple_of(start + half, STEP)
            tpl = g[:, :, pl.ds(at, STEP), :].reshape(GROUP * STEP, LANES)
            term = lax.dot_general(
                xt[slab, pl.ds(at, ROWS), :], tpl, (((1,), (1,)), ((), ())), preferred_element_type=F32
            )
            total = term if total is None else total + term
        if first:
            part[slab, 0:ROWS, :] = total
            part[slab, ROWS:PADDED, :] = jnp.zeros((PADDED - ROWS, GROUP * STEP), F32)
        else:
            part[slab, 0:ROWS, :] += total

    def finish(kind, turn):
        for name, dz, its in plane[kind]:
            if its == turn:
                receive(name, piece(kind, both, dz, turn))

    for kind in (0, 1):
        receive(("cross", kind, 0), piece(kind, other, 0))
        to_line(kind, other, "other")
        if kind == 0:
            receive(("cross", "info"), info.at[other, z])
            to_line("info", other, "other")
    xt[0, 0:SLAB, :] = padded_lanes(wave_v[0].T)
    receive("wave", wave_v.at[1])
    xt[1, 0:SLAB, :] = padded_lanes(wave_v[1].T)
    for step in ((0, 2), (0, -2), ("info", 2), ("info", -2), (0, 1), (0, -1), (1, 2), (1, -2), (1, 1), (1, -1), ("info", 1), ("info", -1)):
        zstep(*step)
    receive("halo", halo_v.at[0])
    send("sib halo", halo_v.at[0], sibling, halo_v.at[1])
    edges = [jnp.where(place == 255, jnp.zeros((), BF16), halo_v[0])]
    xt[0, SLAB:SPAN, :] = padded_lanes(edges[0].T)
    for step in ((0, 3), (0, -3), (0, 4)):
        zstep(*step)
    receive("sib halo", halo_v.at[1])
    edges.append(jnp.where(place + 8 - 16 * core == 255, jnp.zeros((), BF16), halo_v[1]))
    xt[1, SLAB:SPAN, :] = padded_lanes(edges[1].T)
    for turn in (1, 2, 3):
        receive(("cross", 0, turn), piece(0, other, 0, turn))
    for slab in (1, 0):
        multiply(0, 0, slab, True)
    for step in ((1, 3), (1, -3), (1, 4), ("info", 3), ("info", -3), ("info", 4)):
        zstep(*step)

    for turn in (1, 2, 3):
        receive(("cross", 1, turn), piece(1, other, 0, turn))
    gathered = jnp.concatenate(
        [info[:, :, 0, :].reshape(GROUP, 128), info[:, :, 1, :].reshape(GROUP, 128)], axis=1
    ).astype(BF16)
    masks = jnp.dot(gathered, onehot, preferred_element_type=F32).astype(BF16)[:, :CHANNELS]
    gains = info[:, :, 2, :].reshape(GROUP, 128)[:, 0:1]
    for slab in (1, 0):
        total = window_energy(masks, jnp.concatenate([wave_v[slab], edges[slab]], axis=1))
        energy[slab] = gains / jnp.sqrt(total + EPSILON)

    for kind in (0, 1):
        for turn in (0, 2, 1, 3):
            if (kind, turn) != (0, 0):
                finish(kind, turn)
                for slab in (1, 0):
                    multiply(kind, turn, slab)

    result[...] = diagonal_sums(part[1]) * energy[1]
    send("result", result, sibling, arrived)
    out_ref[core] = diagonal_sums(part[0]) * energy[0]
    receive("result", arrived)
    out_ref[1 - core] = arrived[...]
    for made in sent:
        made.wait_send()


def on_device(waveforms, templates, station_mask, channel_order):
    vmem = pl.BlockSpec(memory_space=pltpu.VMEM)
    hbm = pl.BlockSpec(memory_space=pl.ANY)
    slots = 112
    result = pl.pallas_call(
        kernel,
        out_shape=jax.ShapeDtypeStruct((2, GROUP, SLAB), F32),
        in_specs=[hbm] * 4,
        out_specs=vmem,
        scratch_shapes=[
            pltpu.VMEM((2, NZ, WINDOW, LANES), BF16),
            pltpu.VMEM((2, NZ, 8, 128), F32),
            pltpu.VMEM((2, SPAN, LANES), BF16),
            pltpu.VMEM((1, CHANNELS), jnp.int32),
            pltpu.VMEM((1, 160), jnp.int32),
            pltpu.VMEM((CHANNELS, WINDOW), BF16),
            pltpu.VMEM((2, CHANNELS, SLAB), BF16),
            pltpu.VMEM((2, CHANNELS, WINDOW), BF16),
            pltpu.VMEM((2, PADDED, GROUP * STEP), F32),
            pltpu.VMEM((2, GROUP, SLAB), F32),
            pltpu.VMEM((GROUP, SLAB), F32),
            pltpu.VMEM((GROUP, SLAB), F32),
            pltpu.SemaphoreType.DMA((slots,)),
            pltpu.SemaphoreType.DMA((slots,)),
            pltpu.SemaphoreType.DMA((4,)),
        ],
        compiler_params=pltpu.CompilerParams(
            collective_id=0, has_side_effects=True, vmem_limit_bytes=50 * 2**20
        ),
    )(waveforms, templates[0], station_mask, channel_order[None, :])
    return jnp.transpose(result, (1, 0, 2)).reshape(2 * GROUP, SLAB)


def solution(mesh):
    placed = (P(None, ("blk", "tm")), P("blk", None, None), P("blk", None), P())
    return jax.shard_map(
        on_device, mesh=mesh, in_specs=placed, out_specs=P(None, ("blk", "tm")), check_vma=False
    )
```

```python
import jax
import jax.numpy as jnp
from jax import lax
from jax.experimental import pallas as pl
from jax.experimental.pallas import tpu as pltpu
from jax.sharding import PartitionSpec as P

EPSILON = 1e-05
MESH = pl.DeviceIdType.MESH
F32 = jnp.float32
BF16 = jnp.bfloat16

NX, NY, NZ = 4, 4, 8
CHANNELS, WINDOW, SLAB = 480, 256, 512
LANES = 512
SPAN = SLAB + WINDOW
STEP = 16
ROWS = SLAB + STEP
GROUP = 16
PADDED = 640

def padded_lanes(block):
    return jnp.concatenate([block, jnp.zeros((block.shape[0], LANES - block.shape[1]), block.dtype)], axis=1)


def station_onehot(order):
    first = 3 * lax.broadcasted_iota(jnp.int32, (256, CHANNELS), 0)
    hit = jnp.logical_and(order >= first, order < first + 3)
    return padded_lanes(jnp.where(hit, 1.0, 0.0).astype(F32)).astype(BF16)


def window_energy(mask, block):
    wide = block.astype(F32)
    squares = wide * wide
    high = squares.astype(BF16)
    low = (squares - high.astype(F32)).astype(BF16)
    total = jnp.dot(mask, high, preferred_element_type=F32) + jnp.dot(mask, low, preferred_element_type=F32)
    shift = 1
    while shift < WINDOW:
        total = total + pltpu.roll(total, SPAN - shift, 1)
        shift = shift * 2
    return total[:, :SLAB]


def diagonal_sums(partial):
    turned = partial.T.reshape(GROUP, 2, 8, PADDED)
    low, high = turned[:, 0].reshape(GROUP * 8, PADDED), turned[:, 1].reshape(GROUP * 8, PADDED)
    both = low + pltpu.roll(high, PADDED - 8, 1)
    row = lax.broadcasted_iota(jnp.int32, (GROUP * 8, PADDED), 0)
    for bit in (4, 2, 1):
        both = jnp.where((row & bit) != 0, pltpu.roll(both, PADDED - bit, 1), both)
    return jnp.sum(both.reshape(GROUP, 8, PADDED)[:, :, :SLAB], axis=1)


def kernel(
    wave_ref, tpl_ref, flag_ref, order_ref, out_ref,
    g, info, xt, order_v, flag_v, tpl_v, wave_v, halo_v, part, energy, result, arrived, ssem, rsem, lsem,
):
    blk, tm = lax.axis_index("blk"), lax.axis_index("tm")
    core, z, h = blk % 2, (blk // 2) % NZ, blk // 16
    x, low_y = tm % NX, tm // NX
    y = 2 * h + low_y
    other = 1 - h
    colors = ((x + 2 * y) % 4, (2 * x + y) % 4)
    cross_turns = (2, 3 - 2 * low_y)

    def device(px, py, pz, pc):
        px, py, pz = (px + NX) % NX, (py + NY) % NY, (pz + NZ) % NZ
        return ((py // 2 * NZ + pz) * 2 + pc, py % 2 * NX + px)

    line = {dz: device(x, y, z + dz, core) for dz in (1, -1, 2, -2)}
    cross = device(x, y + 2 * low_y - 1, z, core)
    east, west = device(x + 1, y, z, core), device(x - 1, y, z, core)
    north, south = device(x, y + 1, z, core), device(x, y - 1, z, core)
    mate = device(x, y + 1 - 2 * low_y, z, core)
    sibling = device(x, y, z, 1 - core)
    place = blk * 8 + tm
    after, before = (place + 1) % 256, (place + 255) % 256
    after, before = (after // 8, after % 8), (before // 8, before % 8)

    load_tpl = pltpu.make_async_copy(tpl_ref, tpl_v, lsem.at[0])
    load_wave = pltpu.make_async_copy(wave_ref, wave_v.at[0], lsem.at[1])
    load_order = pltpu.make_async_copy(order_ref, order_v, lsem.at[2])
    load_flags = pltpu.make_async_copy(flag_ref, flag_v, lsem.at[3])
    load_order.start()
    load_flags.start()
    load_tpl.start()
    load_wave.start()

    barrier = pltpu.get_barrier_semaphore()
    friends = list(line.values()) + [cross, east, west, mate, sibling, after, before]
    for friend in friends:
        pl.semaphore_signal(barrier, inc=1, device_id=friend, device_id_type=MESH)

    slots, sent = {}, []

    def copy(name, source, target, to):
        slot = slots.setdefault(name, len(slots))
        return pltpu.make_async_remote_copy(
            src_ref=source, dst_ref=target, send_sem=ssem.at[slot], recv_sem=rsem.at[slot], device_id=to, device_id_type=MESH
        )

    def send(name, source, to, target=None):
        made = copy(name, source, source if target is None else target, to)
        made.start()
        sent.append(made)

    def receive(name, target):
        copy(name, target, target, sibling).wait_recv()

    load_order.wait()
    load_flags.wait()
    order = order_v[...]
    onehot = station_onehot(order)
    flags = jnp.concatenate([flag_v[...].astype(F32), jnp.zeros((1, 96), F32)], axis=1)
    mask_row = jnp.dot(jnp.broadcast_to(flags, (16, 256)).astype(BF16), onehot, preferred_element_type=F32)[0:1]
    load_tpl.wait()
    masked = padded_lanes(tpl_v[...].T) * mask_row.astype(BF16)
    g[h, z] = masked
    wide = masked.astype(F32)
    norm = jnp.sum(jnp.sum(wide * wide, axis=0, keepdims=True), axis=1, keepdims=True)
    live = jnp.sum(mask_row, axis=1, keepdims=True)
    scale = jnp.sqrt(WINDOW * live) / jnp.sqrt(norm + EPSILON)
    info[h, z] = jnp.concatenate(
        [flags[:, :128], flags[:, 128:], jnp.broadcast_to(scale, (1, 128)), jnp.zeros((5, 128), F32)], axis=0
    )
    load_wave.wait()
    pl.semaphore_wait(barrier, len(friends))

    def rows(kind, turn):
        return pl.ds(pl.multiple_of(128 * kind + 32 * ((colors[kind] + turn) % 4), 32), 32)

    def piece(kind, hs, dz, turn=0):
        return g.at[hs, (z - dz + NZ) % NZ, rows(kind, turn), :]

    both = pl.ds(0, 2)
    send("halo", wave_v.at[0, :, pl.ds(0, WINDOW)], before, halo_v.at[0])
    send("wave", wave_v.at[0], sibling, wave_v.at[1])
    for kind in (0, 1):
        send(("cross", kind, 0), piece(kind, h, 0, cross_turns[kind]), cross)
    send(("cross", "info"), info.at[h, z], cross)

    sides = {"own": h, "other": other, "info": both}

    def part_of(kind, tag, dz):
        return info.at[both, (z - dz + NZ) % NZ] if kind == "info" else piece(kind, sides[tag], dz)

    def to_line(kind, tag):
        for dz in (2, -2, 1, -1):
            send((kind, tag, dz), part_of(kind, tag, 0), line[dz])

    to_line(0, "own")
    to_line(1, "own")
    for turn in (1, 2, 3):
        for kind in (0, 1):
            send(("cross", kind, turn), piece(kind, h, 0, cross_turns[kind] + turn), cross)

    plane = {0: [], 1: []}

    def zstep(kind, tag, dz):
        receive((kind, tag, dz), part_of(kind, tag, dz))
        sign = 1 if dz > 0 else -1
        if abs(dz) == 2:
            send((kind, tag, 3 * sign), part_of(kind, tag, dz), line[sign])
            if sign == (1 if kind == 0 else -1):
                send((kind, tag, 4), part_of(kind, tag, dz), line[2 * sign])
        if kind == "info":
            return
        if kind == 0:
            pushes = (("east", east, 3), ("west", west, 1), (("cross y", cross, 2) if dz in (2, 1) else ("mate", mate, 2)))
        else:
            third = ("west", west, 2) if dz in (2, -1) else ("east", east, 2)
            pushes = (("north", north, 3), ("south", south, 1), third)
        for label, to, turn in pushes:
            send((kind, label, tag, dz), part_of(kind, tag, dz), to)
            plane[kind].append(((kind, label, tag, dz), sides[tag], dz, turn))

    def multiply(kind, turn, slab, first=False):
        start = 128 * kind + 32 * ((colors[kind] + turn) % 4)
        total = None
        for half in (0, STEP):
            at = pl.multiple_of(start + half, STEP)
            tpl = g[:, :, pl.ds(at, STEP), :].reshape(GROUP * STEP, LANES)
            term = lax.dot_general(
                xt[slab, pl.ds(at, ROWS), :], tpl, (((1,), (1,)), ((), ())), preferred_element_type=F32
            )
            total = term if total is None else total + term
        if first:
            part[slab, 0:ROWS, :] = total
            part[slab, ROWS:PADDED, :] = jnp.zeros((PADDED - ROWS, GROUP * STEP), F32)
        else:
            part[slab, 0:ROWS, :] += total

    def finish(kind, turn):
        for name, side, dz, its in plane[kind]:
            if its == turn:
                receive(name, piece(kind, side, dz, turn))

    near, far = (2, -2, 1, -1), (3, -3, 4)

    def arrive(kind, tag, steps):
        for dz in steps:
            zstep(kind, tag, dz)

    receive(("cross", 0, 0), piece(0, other, 0))
    to_line(0, "other")
    receive(("cross", "info"), info.at[other, z])
    to_line("info", "info")
    receive(("cross", 1, 0), piece(1, other, 0))
    to_line(1, "other")
    arrive(0, "own", near)
    arrive(1, "own", near)
    xt[0, 0:SLAB, :] = padded_lanes(wave_v[0].T)
    receive("wave", wave_v.at[1])
    arrive("info", "info", near)
    arrive(0, "other", near)
    arrive(0, "own", far)
    xt[1, 0:SLAB, :] = padded_lanes(wave_v[1].T)
    arrive(1, "other", near)
    receive("halo", halo_v.at[0])
    send("sib halo", halo_v.at[0], sibling, halo_v.at[1])
    edges = [jnp.where(place == 255, jnp.zeros((), BF16), halo_v[0])]
    xt[0, SLAB:SPAN, :] = padded_lanes(edges[0].T)
    arrive(1, "own", far)
    arrive("info", "info", far)
    gathered = jnp.concatenate(
        [info[:, :, 0, :].reshape(GROUP, 128), info[:, :, 1, :].reshape(GROUP, 128)], axis=1
    ).astype(BF16)
    masks = jnp.dot(gathered, onehot, preferred_element_type=F32).astype(BF16)[:, :CHANNELS]
    gains = info[:, :, 2, :].reshape(GROUP, 128)[:, 0:1]

    def set_energy(slab):
        total = window_energy(masks, jnp.concatenate([wave_v[slab], edges[slab]], axis=1))
        energy[slab] = gains / jnp.sqrt(total + EPSILON)

    set_energy(0)
    arrive(0, "other", far)
    arrive(1, "other", far)
    for turn in (1, 2, 3):
        receive(("cross", 0, turn), piece(0, other, 0, turn))
        receive(("cross", 1, turn), piece(1, other, 0, turn))
    multiply(0, 0, 0, True)
    receive("sib halo", halo_v.at[1])
    edges.append(jnp.where(place + 8 - 16 * core == 255, jnp.zeros((), BF16), halo_v[1]))
    xt[1, SLAB:SPAN, :] = padded_lanes(edges[1].T)
    multiply(0, 0, 1, True)
    set_energy(1)
    chunks = [(kind, turn) for kind in (0, 1) for turn in (0, 2, 1, 3)]
    for kind, turn in chunks[1:-1]:
        finish(kind, turn)
        for slab in (1, 0):
            multiply(kind, turn, slab)
    finish(*chunks[-1])
    multiply(*chunks[-1], 1)
    result[...] = diagonal_sums(part[1]) * energy[1]
    send("result", result, sibling, arrived)
    multiply(*chunks[-1], 0)
    own = diagonal_sums(part[0]) * energy[0]
    for i in range(GROUP):
        out_ref[pl.ds(2 * i + core, 1), :] = own[i : i + 1]
    receive("result", arrived)
    for i in range(GROUP):
        out_ref[pl.ds(2 * i + 1 - core, 1), :] = arrived[i : i + 1, :]
    for made in sent:
        made.wait_send()


def on_device(waveforms, templates, station_mask, channel_order):
    vmem = pl.BlockSpec(memory_space=pltpu.VMEM)
    hbm = pl.BlockSpec(memory_space=pl.ANY)
    slots = 160
    return pl.pallas_call(
        kernel,
        out_shape=jax.ShapeDtypeStruct((2 * GROUP, SLAB), F32),
        in_specs=[hbm] * 4,
        out_specs=vmem,
        scratch_shapes=[
            pltpu.VMEM((2, NZ, WINDOW, LANES), BF16),
            pltpu.VMEM((2, NZ, 8, 128), F32),
            pltpu.VMEM((2, SPAN, LANES), BF16),
            pltpu.VMEM((1, CHANNELS), jnp.int32),
            pltpu.VMEM((1, 160), jnp.int32),
            pltpu.VMEM((CHANNELS, WINDOW), BF16),
            pltpu.VMEM((2, CHANNELS, SLAB), BF16),
            pltpu.VMEM((2, CHANNELS, WINDOW), BF16),
            pltpu.VMEM((2, PADDED, GROUP * STEP), F32),
            pltpu.VMEM((2, GROUP, SLAB), F32),
            pltpu.VMEM((GROUP, SLAB), F32),
            pltpu.VMEM((GROUP, SLAB), F32),
            pltpu.SemaphoreType.DMA((slots,)),
            pltpu.SemaphoreType.DMA((slots,)),
            pltpu.SemaphoreType.DMA((4,)),
        ],
        compiler_params=pltpu.CompilerParams(
            collective_id=0, has_side_effects=True, vmem_limit_bytes=67_043_328
        ),
    )(waveforms, templates[0], station_mask, channel_order[None, :])


def solution(mesh):
    placed = (P(None, ("blk", "tm")), P("blk", None, None), P("blk", None), P())
    return jax.shard_map(
        on_device, mesh=mesh, in_specs=placed, out_specs=P(None, ("blk", "tm")), check_vma=False
    )
```

```python
import jax
import jax.numpy as jnp
from jax import lax
from jax.experimental import pallas as pl
from jax.experimental.pallas import tpu as pltpu
from jax.sharding import PartitionSpec as P

EPSILON = 1e-05
MESH = pl.DeviceIdType.MESH
F32 = jnp.float32
BF16 = jnp.bfloat16

NX, NY, NZ = 4, 4, 8
CHANNELS, WINDOW, SLAB = 480, 256, 512
LANES = 512
SPAN = SLAB + WINDOW
STEP = 16
ROWS = SLAB + STEP
GROUP = 16
PADDED = 640

def padded_lanes(block):
    return jnp.concatenate([block, jnp.zeros((block.shape[0], LANES - block.shape[1]), block.dtype)], axis=1)


def station_onehot(order):
    first = 3 * lax.broadcasted_iota(jnp.int32, (256, CHANNELS), 0)
    hit = jnp.logical_and(order >= first, order < first + 3)
    return padded_lanes(jnp.where(hit, 1.0, 0.0).astype(F32)).astype(BF16)


def window_energy(mask, block):
    wide = block.astype(F32)
    squares = wide * wide
    high = squares.astype(BF16)
    low = (squares - high.astype(F32)).astype(BF16)
    total = jnp.dot(mask, high, preferred_element_type=F32) + jnp.dot(mask, low, preferred_element_type=F32)
    shift = 1
    while shift < WINDOW:
        total = total + pltpu.roll(total, SPAN - shift, 1)
        shift = shift * 2
    return total[:, :SLAB]


def diagonal_sums(partial):
    turned = partial.T.reshape(GROUP, 2, 8, PADDED)
    low, high = turned[:, 0].reshape(GROUP * 8, PADDED), turned[:, 1].reshape(GROUP * 8, PADDED)
    both = low + pltpu.roll(high, PADDED - 8, 1)
    row = lax.broadcasted_iota(jnp.int32, (GROUP * 8, PADDED), 0)
    for bit in (4, 2, 1):
        both = jnp.where((row & bit) != 0, pltpu.roll(both, PADDED - bit, 1), both)
    return jnp.sum(both.reshape(GROUP, 8, PADDED)[:, :, :SLAB], axis=1)


def kernel(
    wave_ref, tpl_ref, flag_ref, order_ref, out_ref,
    g, info, xt, order_v, flag_v, tpl_v, wave_v, halo_v, part, energy, result, arrived, ssem, rsem, lsem,
):
    blk, tm = lax.axis_index("blk"), lax.axis_index("tm")
    core, z, h = blk % 2, (blk // 2) % NZ, blk // 16
    x, low_y = tm % NX, tm // NX
    y = 2 * h + low_y
    other = 1 - h
    colors = ((x + 2 * y) % 4, (2 * x + y) % 4)
    cross_turns = (2, 3 - 2 * low_y)

    def device(px, py, pz, pc):
        px, py, pz = (px + NX) % NX, (py + NY) % NY, (pz + NZ) % NZ
        return ((py // 2 * NZ + pz) * 2 + pc, py % 2 * NX + px)

    line = {dz: device(x, y, z + dz, core) for dz in (1, -1, 2, -2)}
    cross = device(x, y + 2 * low_y - 1, z, core)
    east, west = device(x + 1, y, z, core), device(x - 1, y, z, core)
    north, south = device(x, y + 1, z, core), device(x, y - 1, z, core)
    mate = device(x, y + 1 - 2 * low_y, z, core)
    sibling = device(x, y, z, 1 - core)
    place = blk * 8 + tm
    after, before = (place + 1) % 256, (place + 255) % 256
    after, before = (after // 8, after % 8), (before // 8, before % 8)

    load_tpl = pltpu.make_async_copy(tpl_ref, tpl_v, lsem.at[0])
    load_wave = pltpu.make_async_copy(wave_ref, wave_v.at[0], lsem.at[1])
    load_order = pltpu.make_async_copy(order_ref, order_v, lsem.at[2])
    load_flags = pltpu.make_async_copy(flag_ref, flag_v, lsem.at[3])
    load_order.start()
    load_flags.start()
    load_tpl.start()
    load_wave.start()

    barrier = pltpu.get_barrier_semaphore()
    friends = list(line.values()) + [cross, east, west, mate, sibling, after, before]
    for friend in friends:
        pl.semaphore_signal(barrier, inc=1, device_id=friend, device_id_type=MESH)

    slots, sent = {}, []

    def copy(name, source, target, to):
        slot = slots.setdefault(name, len(slots))
        return pltpu.make_async_remote_copy(
            src_ref=source, dst_ref=target, send_sem=ssem.at[slot], recv_sem=rsem.at[slot], device_id=to, device_id_type=MESH
        )

    def send(name, source, to, target=None):
        made = copy(name, source, source if target is None else target, to)
        made.start()
        sent.append(made)

    def receive(name, target):
        copy(name, target, target, sibling).wait_recv()

    load_order.wait()
    load_flags.wait()
    order = order_v[...]
    onehot = station_onehot(order)
    flags = jnp.concatenate([flag_v[...].astype(F32), jnp.zeros((1, 96), F32)], axis=1)
    mask_row = jnp.dot(jnp.broadcast_to(flags, (16, 256)).astype(BF16), onehot, preferred_element_type=F32)[0:1]
    load_wave.wait()
    pl.semaphore_wait(barrier, len(friends))
    send("halo", wave_v.at[0, :, pl.ds(0, WINDOW)], before, halo_v.at[0])
    send("wave", wave_v.at[0], sibling, wave_v.at[1])
    load_tpl.wait()
    masked = padded_lanes(tpl_v[...].T) * mask_row.astype(BF16)
    g[h, z] = masked
    def rows(kind, turn):
        return pl.ds(pl.multiple_of(128 * kind + 32 * ((colors[kind] + turn) % 4), 32), 32)

    def piece(kind, hs, dz, turn=0):
        return g.at[hs, (z - dz + NZ) % NZ, rows(kind, turn), :]

    both = pl.ds(0, 2)
    for kind in (0, 1):
        send(("cross", kind, 0), piece(kind, h, 0, cross_turns[kind]), cross)

    sides = {"own": h, "other": other, "info": both}

    def part_of(kind, tag, dz):
        return info.at[both, (z - dz + NZ) % NZ] if kind == "info" else piece(kind, sides[tag], dz)

    def to_line(kind, tag):
        for dz in (2, -2, 1, -1):
            send((kind, tag, dz), part_of(kind, tag, 0), line[dz])

    to_line(0, "own")
    to_line(1, "own")
    wide = masked.astype(F32)
    norm = jnp.sum(jnp.sum(wide * wide, axis=0, keepdims=True), axis=1, keepdims=True)
    live = jnp.sum(mask_row, axis=1, keepdims=True)
    scale = jnp.sqrt(WINDOW * live) / jnp.sqrt(norm + EPSILON)
    info[h, z] = jnp.concatenate(
        [flags[:, :128], flags[:, 128:], jnp.broadcast_to(scale, (1, 128)), jnp.zeros((5, 128), F32)], axis=0
    )
    send(("cross", "info"), info.at[h, z], cross)
    for turn in (1, 2, 3):
        for kind in (0, 1):
            send(("cross", kind, turn), piece(kind, h, 0, cross_turns[kind] + turn), cross)

    plane = {0: [], 1: []}

    def zstep(kind, tag, dz):
        receive((kind, tag, dz), part_of(kind, tag, dz))
        sign = 1 if dz > 0 else -1
        if abs(dz) == 2:
            send((kind, tag, 3 * sign), part_of(kind, tag, dz), line[sign])
            if sign == (1 if kind == 0 else -1):
                send((kind, tag, 4), part_of(kind, tag, dz), line[2 * sign])
        if kind == "info":
            return
        if kind == 0:
            pushes = (("east", east, 3), ("west", west, 1), (("cross y", cross, 2) if dz in (-3, 4) else ("mate", mate, 2)))
        else:
            third = ("west", west, 2) if dz in (-3, 4, -1) else ("east", east, 2)
            pushes = (("north", north, 3), ("south", south, 1), third)
        for label, to, turn in pushes:
            send((kind, label, tag, dz), part_of(kind, tag, dz), to)
            plane[kind].append(((kind, label, tag, dz), sides[tag], dz, turn))

    def multiply(kind, turn, slab, first=False):
        start = 128 * kind + 32 * ((colors[kind] + turn) % 4)
        total = None
        for half in (0, STEP):
            at = pl.multiple_of(start + half, STEP)
            tpl = g[:, :, pl.ds(at, STEP), :].reshape(GROUP * STEP, LANES)
            term = lax.dot_general(
                xt[slab, pl.ds(at, ROWS), :], tpl, (((1,), (1,)), ((), ())), preferred_element_type=F32
            )
            total = term if total is None else total + term
        if first:
            part[slab, 0:ROWS, :] = total
            part[slab, ROWS:PADDED, :] = jnp.zeros((PADDED - ROWS, GROUP * STEP), F32)
        else:
            part[slab, 0:ROWS, :] += total

    def finish(kind, turn):
        for name, side, dz, its in plane[kind]:
            if its == turn:
                receive(name, piece(kind, side, dz, turn))

    near, far = (2, -2, 1, -1), (3, -3, 4)

    def arrive(kind, tag, steps):
        for dz in steps:
            zstep(kind, tag, dz)

    receive(("cross", 0, 0), piece(0, other, 0))
    to_line(0, "other")
    receive(("cross", "info"), info.at[other, z])
    to_line("info", "info")
    receive(("cross", 1, 0), piece(1, other, 0))
    to_line(1, "other")
    arrive(0, "own", near)
    arrive(1, "own", near)
    xt[0, 0:SLAB, :] = padded_lanes(wave_v[0].T)
    receive("wave", wave_v.at[1])
    arrive("info", "info", near)
    arrive(0, "other", near)
    xt[1, 0:SLAB, :] = padded_lanes(wave_v[1].T)
    arrive(1, "other", near)
    arrive(0, "own", far)
    receive("halo", halo_v.at[0])
    send("sib halo", halo_v.at[0], sibling, halo_v.at[1])
    edges = [jnp.where(place == 255, jnp.zeros((), BF16), halo_v[0])]
    xt[0, SLAB:SPAN, :] = padded_lanes(edges[0].T)
    arrive(1, "own", far)
    arrive("info", "info", far)
    gathered = jnp.concatenate(
        [info[:, :, 0, :].reshape(GROUP, 128), info[:, :, 1, :].reshape(GROUP, 128)], axis=1
    ).astype(BF16)
    masks = jnp.dot(gathered, onehot, preferred_element_type=F32).astype(BF16)[:, :CHANNELS]
    gains = info[:, :, 2, :].reshape(GROUP, 128)[:, 0:1]

    def set_energy(slab):
        total = window_energy(masks, jnp.concatenate([wave_v[slab], edges[slab]], axis=1))
        energy[slab] = gains / jnp.sqrt(total + EPSILON)

    set_energy(0)
    arrive(0, "other", far)
    early = len(sent)
    arrive(1, "other", far)
    for turn in (1, 2, 3):
        receive(("cross", 0, turn), piece(0, other, 0, turn))
        receive(("cross", 1, turn), piece(1, other, 0, turn))
    multiply(0, 0, 0, True)
    receive("sib halo", halo_v.at[1])
    edges.append(jnp.where(place + 8 - 16 * core == 255, jnp.zeros((), BF16), halo_v[1]))
    xt[1, SLAB:SPAN, :] = padded_lanes(edges[1].T)
    multiply(0, 0, 1, True)
    set_energy(1)
    chunks = [(kind, turn) for kind in (0, 1) for turn in (0, 2, 1, 3)]
    for kind, turn in chunks[1:-1]:
        if (kind, turn) == (1, 2):
            for made in sent[:early]:
                made.wait_send()
        finish(kind, turn)
        for slab in (1, 0):
            multiply(kind, turn, slab)
    finish(*chunks[-1])
    multiply(*chunks[-1], 1)
    result[...] = diagonal_sums(part[1]) * energy[1]
    send("result", result, sibling, arrived)
    multiply(*chunks[-1], 0)
    own = diagonal_sums(part[0]) * energy[0]
    for i in range(GROUP):
        out_ref[pl.ds(2 * i + core, 1), :] = own[i : i + 1]
    receive("result", arrived)
    for i in range(GROUP):
        out_ref[pl.ds(2 * i + 1 - core, 1), :] = arrived[i : i + 1, :]
    for made in sent[early:]:
        made.wait_send()


def on_device(waveforms, templates, station_mask, channel_order):
    vmem = pl.BlockSpec(memory_space=pltpu.VMEM)
    hbm = pl.BlockSpec(memory_space=pl.ANY)
    slots = 160
    return pl.pallas_call(
        kernel,
        out_shape=jax.ShapeDtypeStruct((2 * GROUP, SLAB), F32),
        in_specs=[hbm] * 4,
        out_specs=vmem,
        scratch_shapes=[
            pltpu.VMEM((2, NZ, WINDOW, LANES), BF16),
            pltpu.VMEM((2, NZ, 8, 128), F32),
            pltpu.VMEM((2, SPAN, LANES), BF16),
            pltpu.VMEM((1, CHANNELS), jnp.int32),
            pltpu.VMEM((1, 160), jnp.int32),
            pltpu.VMEM((CHANNELS, WINDOW), BF16),
            pltpu.VMEM((2, CHANNELS, SLAB), BF16),
            pltpu.VMEM((2, CHANNELS, WINDOW), BF16),
            pltpu.VMEM((2, PADDED, GROUP * STEP), F32),
            pltpu.VMEM((2, GROUP, SLAB), F32),
            pltpu.VMEM((GROUP, SLAB), F32),
            pltpu.VMEM((GROUP, SLAB), F32),
            pltpu.SemaphoreType.DMA((slots,)),
            pltpu.SemaphoreType.DMA((slots,)),
            pltpu.SemaphoreType.DMA((4,)),
        ],
        compiler_params=pltpu.CompilerParams(
            collective_id=0, has_side_effects=True, vmem_limit_bytes=67_043_328
        ),
    )(waveforms, templates[0], station_mask, channel_order[None, :])


def solution(mesh):
    placed = (P(None, ("blk", "tm")), P("blk", None, None), P("blk", None), P())
    return jax.shard_map(
        on_device, mesh=mesh, in_specs=placed, out_specs=P(None, ("blk", "tm")), check_vma=False
    )
```

```python
import jax
import jax.numpy as jnp
from jax import lax
from jax.experimental import pallas as pl
from jax.experimental.pallas import tpu as pltpu
from jax.sharding import PartitionSpec as P

EPSILON = 1e-05
MESH = pl.DeviceIdType.MESH
F32 = jnp.float32
BF16 = jnp.bfloat16

NX, NY, NZ = 4, 4, 8
CHANNELS, WINDOW, SLAB = 480, 256, 512
LANES = 512
SPAN = SLAB + WINDOW
STEP = 16
ROWS = SLAB + STEP
GROUP = 16
PADDED = 640

def padded_lanes(block):
    return jnp.concatenate([block, jnp.zeros((block.shape[0], LANES - block.shape[1]), block.dtype)], axis=1)


def station_onehot(order):
    first = 3 * lax.broadcasted_iota(jnp.int32, (256, CHANNELS), 0)
    hit = jnp.logical_and(order >= first, order < first + 3)
    return padded_lanes(jnp.where(hit, 1.0, 0.0).astype(F32)).astype(BF16)


def window_energy(mask, block):
    wide = block.astype(F32)
    squares = wide * wide
    high = squares.astype(BF16)
    low = (squares - high.astype(F32)).astype(BF16)
    total = jnp.dot(mask, high, preferred_element_type=F32) + jnp.dot(mask, low, preferred_element_type=F32)
    shift = 1
    while shift < WINDOW:
        total = total + pltpu.roll(total, SPAN - shift, 1)
        shift = shift * 2
    return total[:, :SLAB]


def diagonal_sums(partial):
    turned = partial.T.reshape(GROUP, 2, 8, PADDED)
    low, high = turned[:, 0].reshape(GROUP * 8, PADDED), turned[:, 1].reshape(GROUP * 8, PADDED)
    both = low + pltpu.roll(high, PADDED - 8, 1)
    row = lax.broadcasted_iota(jnp.int32, (GROUP * 8, PADDED), 0)
    for bit in (4, 2, 1):
        both = jnp.where((row & bit) != 0, pltpu.roll(both, PADDED - bit, 1), both)
    return jnp.sum(both.reshape(GROUP, 8, PADDED)[:, :, :SLAB], axis=1)


def kernel(
    wave_ref, tpl_ref, flag_ref, order_ref, out_ref,
    g, info, xt, order_v, flag_v, tpl_v, wave_v, halo_v, part, energy, result, arrived, ssem, rsem, lsem,
):
    blk, tm = lax.axis_index("blk"), lax.axis_index("tm")
    core, z, h = blk % 2, (blk // 2) % NZ, blk // 16
    x, low_y = tm % NX, tm // NX
    y = 2 * h + low_y
    other = 1 - h
    colors = ((x + 2 * y) % 4, (2 * x + y) % 4)
    cross_turns = (2, 3 - 2 * low_y)

    def device(px, py, pz, pc):
        px, py, pz = (px + NX) % NX, (py + NY) % NY, (pz + NZ) % NZ
        return ((py // 2 * NZ + pz) * 2 + pc, py % 2 * NX + px)

    line = {dz: device(x, y, z + dz, core) for dz in (1, -1, 2, -2)}
    cross = device(x, y + 2 * low_y - 1, z, core)
    east, west = device(x + 1, y, z, core), device(x - 1, y, z, core)
    north, south = device(x, y + 1, z, core), device(x, y - 1, z, core)
    mate = device(x, y + 1 - 2 * low_y, z, core)
    sibling = device(x, y, z, 1 - core)
    place = blk * 8 + tm
    after, before = (place + 1) % 256, (place + 255) % 256
    after, before = (after // 8, after % 8), (before // 8, before % 8)

    load_tpl = pltpu.make_async_copy(tpl_ref, tpl_v, lsem.at[0])
    load_wave = pltpu.make_async_copy(wave_ref, wave_v.at[0], lsem.at[1])
    load_order = pltpu.make_async_copy(order_ref, order_v, lsem.at[2])
    load_flags = pltpu.make_async_copy(flag_ref, flag_v, lsem.at[3])
    load_order.start()
    load_flags.start()
    load_tpl.start()
    load_wave.start()

    barrier = pltpu.get_barrier_semaphore()
    friends = list(line.values()) + [cross, east, west, mate, sibling, after, before]
    for friend in friends:
        pl.semaphore_signal(barrier, inc=1, device_id=friend, device_id_type=MESH)

    slots, sent = {}, []

    def copy(name, source, target, to):
        slot = slots.setdefault(name, len(slots))
        return pltpu.make_async_remote_copy(
            src_ref=source, dst_ref=target, send_sem=ssem.at[slot], recv_sem=rsem.at[slot], device_id=to, device_id_type=MESH
        )

    def send(name, source, to, target=None):
        made = copy(name, source, source if target is None else target, to)
        made.start()
        sent.append(made)

    def receive(name, target):
        copy(name, target, target, sibling).wait_recv()

    load_order.wait()
    load_flags.wait()
    order = order_v[...]
    onehot = station_onehot(order)
    flags = jnp.concatenate([flag_v[...].astype(F32), jnp.zeros((1, 96), F32)], axis=1)
    mask_row = jnp.dot(jnp.broadcast_to(flags, (16, 256)).astype(BF16), onehot, preferred_element_type=F32)[0:1]
    load_wave.wait()
    pl.semaphore_wait(barrier, len(friends))
    send("halo", wave_v.at[0, :, pl.ds(0, WINDOW)], before, halo_v.at[0])
    send("wave", wave_v.at[0], sibling, wave_v.at[1])
    load_tpl.wait()
    masked = padded_lanes(tpl_v[...].T) * mask_row.astype(BF16)
    g[h, z] = masked
    def rows(kind, turn):
        return pl.ds(pl.multiple_of(128 * kind + 32 * ((colors[kind] + turn) % 4), 32), 32)

    def piece(kind, hs, dz, turn=0):
        return g.at[hs, (z - dz + NZ) % NZ, rows(kind, turn), :]

    both = pl.ds(0, 2)
    for kind in (0, 1):
        send(("cross", kind, 0), piece(kind, h, 0, cross_turns[kind]), cross)

    sides = {"own": h, "other": other, "info": both}

    def part_of(kind, tag, dz):
        return info.at[both, (z - dz + NZ) % NZ] if kind == "info" else piece(kind, sides[tag], dz)

    def to_line(kind, tag):
        for dz in (2, -2, 1, -1):
            send((kind, tag, dz), part_of(kind, tag, 0), line[dz])

    to_line(0, "own")
    to_line(1, "own")
    wide = masked.astype(F32)
    norm = jnp.sum(jnp.sum(wide * wide, axis=0, keepdims=True), axis=1, keepdims=True)
    live = jnp.sum(mask_row, axis=1, keepdims=True)
    scale = jnp.sqrt(WINDOW * live) / jnp.sqrt(norm + EPSILON)
    info[h, z] = jnp.concatenate(
        [flags[:, :128], flags[:, 128:], jnp.broadcast_to(scale, (1, 128)), jnp.zeros((5, 128), F32)], axis=0
    )
    send(("cross", "info"), info.at[h, z], cross)
    for turn in (1, 2, 3):
        for kind in (0, 1):
            send(("cross", kind, turn), piece(kind, h, 0, cross_turns[kind] + turn), cross)

    plane = {0: [], 1: []}

    def zstep(kind, tag, dz):
        receive((kind, tag, dz), part_of(kind, tag, dz))
        sign = 1 if dz > 0 else -1
        if abs(dz) == 2:
            send((kind, tag, 3 * sign), part_of(kind, tag, dz), line[sign])
            if sign == (1 if kind == 0 else -1):
                send((kind, tag, 4), part_of(kind, tag, dz), line[2 * sign])
        if kind == "info":
            return
        if kind == 0:
            pushes = (("east", east, 3), ("west", west, 1), (("cross y", cross, 2) if dz in (-3, 4) else ("mate", mate, 2)))
        else:
            third = ("west", west, 2) if dz in (-3, 4, -1) else ("east", east, 2)
            pushes = (("north", north, 3), ("south", south, 1), third)
        for label, to, turn in pushes:
            send((kind, label, tag, dz), part_of(kind, tag, dz), to)
            plane[kind].append(((kind, label, tag, dz), sides[tag], dz, turn))

    def multiply(kind, turn, slab, first=False, last=False):
        start = 128 * kind + 32 * ((colors[kind] + turn) % 4)
        total = None
        for half in (0, STEP):
            at = pl.multiple_of(start + half, STEP)
            tpl = g[:, :, pl.ds(at, STEP), :].reshape(GROUP * STEP, LANES)
            term = lax.dot_general(
                xt[slab, pl.ds(at, ROWS), :], tpl, (((1,), (1,)), ((), ())), preferred_element_type=F32
            )
            total = term if total is None else total + term
        if last:
            rest = jnp.zeros((PADDED - ROWS, GROUP * STEP), F32)
            return diagonal_sums(jnp.concatenate([part[slab, 0:ROWS, :] + total, rest], axis=0)) * energy[slab]
        if first:
            part[slab, 0:ROWS, :] = total
        else:
            part[slab, 0:ROWS, :] += total

    def finish(kind, turn):
        for name, side, dz, its in plane[kind]:
            if its == turn:
                receive(name, piece(kind, side, dz, turn))

    near, far = (2, -2, 1, -1), (3, -3, 4)

    def arrive(kind, tag, steps):
        for dz in steps:
            zstep(kind, tag, dz)

    receive(("cross", 0, 0), piece(0, other, 0))
    to_line(0, "other")
    receive(("cross", "info"), info.at[other, z])
    to_line("info", "info")
    receive(("cross", 1, 0), piece(1, other, 0))
    to_line(1, "other")
    arrive(0, "own", near)
    arrive(1, "own", near)
    xt[0, 0:SLAB, :] = padded_lanes(wave_v[0].T)
    receive("wave", wave_v.at[1])
    arrive("info", "info", near)
    arrive(0, "other", near)
    xt[1, 0:SLAB, :] = padded_lanes(wave_v[1].T)
    arrive(1, "other", near)
    arrive(0, "own", far)
    receive("halo", halo_v.at[0])
    send("sib halo", halo_v.at[0], sibling, halo_v.at[1])
    edges = [jnp.where(place == 255, jnp.zeros((), BF16), halo_v[0])]
    xt[0, SLAB:SPAN, :] = padded_lanes(edges[0].T)
    arrive(1, "own", far)
    arrive("info", "info", far)
    gathered = jnp.concatenate(
        [info[:, :, 0, :].reshape(GROUP, 128), info[:, :, 1, :].reshape(GROUP, 128)], axis=1
    ).astype(BF16)
    masks = jnp.dot(gathered, onehot, preferred_element_type=F32).astype(BF16)[:, :CHANNELS]
    gains = info[:, :, 2, :].reshape(GROUP, 128)[:, 0:1]

    def set_energy(slab):
        total = window_energy(masks, jnp.concatenate([wave_v[slab], edges[slab]], axis=1))
        energy[slab] = gains / jnp.sqrt(total + EPSILON)

    set_energy(0)
    arrive(0, "other", far)
    early = len(sent)
    arrive(1, "other", far)
    for turn in (1, 2, 3):
        receive(("cross", 0, turn), piece(0, other, 0, turn))
        receive(("cross", 1, turn), piece(1, other, 0, turn))
    multiply(0, 0, 0, True)
    receive("sib halo", halo_v.at[1])
    edges.append(jnp.where(place + 8 - 16 * core == 255, jnp.zeros((), BF16), halo_v[1]))
    xt[1, SLAB:SPAN, :] = padded_lanes(edges[1].T)
    multiply(0, 0, 1, True)
    set_energy(1)
    chunks = [(kind, turn) for kind in (0, 1) for turn in (0, 2, 1, 3)]
    for kind, turn in chunks[1:-1]:
        if (kind, turn) == (1, 2):
            for made in sent[:early]:
                made.wait_send()
        finish(kind, turn)
        for slab in (1, 0):
            multiply(kind, turn, slab)
    finish(*chunks[-1])
    result[...] = multiply(*chunks[-1], 1, last=True)
    send("result", result, sibling, arrived)
    own = multiply(*chunks[-1], 0, last=True)
    for i in range(GROUP):
        out_ref[pl.ds(2 * i + core, 1), :] = own[i : i + 1]
    receive("result", arrived)
    for i in range(GROUP):
        out_ref[pl.ds(2 * i + 1 - core, 1), :] = arrived[i : i + 1, :]
    for made in sent[early:]:
        made.wait_send()


def on_device(waveforms, templates, station_mask, channel_order):
    vmem = pl.BlockSpec(memory_space=pltpu.VMEM)
    hbm = pl.BlockSpec(memory_space=pl.ANY)
    slots = 160
    return pl.pallas_call(
        kernel,
        out_shape=jax.ShapeDtypeStruct((2 * GROUP, SLAB), F32),
        in_specs=[hbm] * 4,
        out_specs=vmem,
        scratch_shapes=[
            pltpu.VMEM((2, NZ, WINDOW, LANES), BF16),
            pltpu.VMEM((2, NZ, 8, 128), F32),
            pltpu.VMEM((2, SPAN, LANES), BF16),
            pltpu.VMEM((1, CHANNELS), jnp.int32),
            pltpu.VMEM((1, 160), jnp.int32),
            pltpu.VMEM((CHANNELS, WINDOW), BF16),
            pltpu.VMEM((2, CHANNELS, SLAB), BF16),
            pltpu.VMEM((2, CHANNELS, WINDOW), BF16),
            pltpu.VMEM((2, PADDED, GROUP * STEP), F32),
            pltpu.VMEM((2, GROUP, SLAB), F32),
            pltpu.VMEM((GROUP, SLAB), F32),
            pltpu.VMEM((GROUP, SLAB), F32),
            pltpu.SemaphoreType.DMA((slots,)),
            pltpu.SemaphoreType.DMA((slots,)),
            pltpu.SemaphoreType.DMA((4,)),
        ],
        compiler_params=pltpu.CompilerParams(
            collective_id=0, has_side_effects=True, vmem_limit_bytes=67_043_328
        ),
    )(waveforms, templates[0], station_mask, channel_order[None, :])


def solution(mesh):
    placed = (P(None, ("blk", "tm")), P("blk", None, None), P("blk", None), P())
    return jax.shard_map(
        on_device, mesh=mesh, in_specs=placed, out_specs=P(None, ("blk", "tm")), check_vma=False
    )
```
